256 devices in a mesh: row: 16 (over x, z_lo), col: 16 (over y, z_hi, core).
Axes of the slice: x: 4, y: 4, z: 8 (z_hi: 2, z_lo: 4; z = z_hi * 4 + z_lo), core: 2. Of those that a mesh axis runs over, the one named last changes fastest.
Arguments:
- state: bfloat16 [256, 32768], P(None, ('row', 'col')), may hold values from -0.94921875 to 0.94921875
- adjoint: bfloat16 [256, 32768], P(None, ('col', 'row')), may hold values from -6 to 6
- features: bfloat16 [128, 32768], P(None, ('col', 'row')), may hold values from -6 to 6
- cotangent: bfloat16 [256, 32768], P(None, ('row', 'col')), may hold values from -6 to 6
- mixing: bfloat16 [256, 256], replicated, may hold values from -0.375 to 0.375
- input_weight: bfloat16 [256, 128], replicated, may hold values from -0.5 to 0.5
- tiles: bfloat16 [16, 16, 85, 128, 128], P('row', 'col'), may hold values from -0.0625 to 0.0625
- tile_rows: int32 [16, 16, 85], P('row', 'col'), may hold values from 0 to 15, as said below
- tile_cols: int32 [16, 16, 85], P('row', 'col'), may hold values from 0 to 15, as said below
- live_tiles: int32 [16, 16], P('row', 'col'), may hold values from 42 to 85, as said below
Outputs:
- new_state: bfloat16 [256, 32768], P(None, ('col', 'row'))
- new_adjoint: bfloat16 [256, 32768], P(None, ('row', 'col'))
The draws below stay inside these ranges and needn't reach their ends.
Inputs may be any that keep to these rules, and one draw needn't show every extreme that they name: On one device the pairs (tile_rows, tile_cols) of its 85 slots are all different. `tile_cols`: see tile_rows. `live_tiles`: some device has all 85 slots live.
All inputs are finite; a program needn't handle non-finite values.
Results may differ from the reference program's by a relative error of at most 0.014.
Values may be sent and summed in bfloat16 or wider, within the bound.
A program may use at most 64 MiB of HBM per device.

```python
import jax
import jax.numpy as jnp
from jax import lax

H = 256
F = 128
TILE = 128
BR = 16
BC = 16
N = 32768
CAP = 85
N_ROW = 16
N_COL = 16


def pattern(key):
    row_count = N // (BR * TILE)
    col_count = N // (BC * TILE)
    total = BR * BC
    first_key = jax.random.fold_in(key, 101)
    second_key = jax.random.fold_in(key, 202)
    third_key = jax.random.fold_in(key, 303)
    scores = jax.random.randint(first_key, (row_count, col_count, total), 0, 2 ** 30 // total, dtype=jnp.int32)
    scores = scores * total + jnp.arange(total, dtype=jnp.int32)
    chosen = jnp.argsort(scores, axis=-1)[..., :CAP].astype(jnp.int32)
    rows_drawn = chosen // BC
    cols_drawn = chosen % BC
    counts = jax.random.randint(second_key, (row_count, col_count), CAP // 2, CAP + 1, dtype=jnp.int32)
    fullest = jax.random.randint(third_key, (), 0, row_count * col_count, dtype=jnp.int32)
    places = jnp.arange(row_count * col_count, dtype=jnp.int32).reshape(row_count, col_count)
    counts = jnp.where(places == fullest, CAP, counts)
    return (rows_drawn, cols_drawn, counts)


def draw_tile_rows(key, part):
    return pattern(key)[0].astype(jnp.int32)


def draw_tile_cols(key, part):
    return pattern(key)[1].astype(jnp.int32)


def draw_live_tiles(key, part):
    return pattern(key)[2].astype(jnp.int32)


def levels(stream_key, dims, split, smallest, high):
    factor_of, own = 1.0, jax.random.fold_in(stream_key, 6)
    for position, blocks in split:
        draws = jnp.exp(jax.random.uniform(jax.random.fold_in(own, position), (blocks,), jnp.float32, smallest / len(split), high / len(split)))
        factor_of = factor_of * jnp.repeat(draws, dims[position] // blocks).reshape([-1 if axis == position else 1 for axis in range(len(dims))])
    return factor_of


def scatter_about(rng, shape, spread, reach, shards=(), kind=jnp.bfloat16):
    array = jax.random.normal(rng, shape, jnp.float32) * spread
    if len(shards) > 0:
        array = levels(rng, shape, shards, -0.22, 0.18) * array
    return jnp.clip(array, min=-reach, max=reach).astype(kind)


def setup_inputs(seed: int = 0) -> dict:
    arg_keys = jax.random.split(jax.random.key(seed), 11)
    return {
        "state": jnp.clip(jax.random.uniform(arg_keys[0], (H, N), jnp.float32, -0.94921875, 0.94921875) * levels(arg_keys[0], (H, N), ((1, 256),), -0.4, 0.0), -0.94921875, 0.94921875).astype(jnp.bfloat16),
        "adjoint": scatter_about(arg_keys[1], (H, N), 1.0, 6.0, ((1, 256),)),
        "features": scatter_about(arg_keys[2], (F, N), 1.0, 6.0, ((1, 256),)),
        "cotangent": scatter_about(arg_keys[3], (H, N), 1.0, 6.0, ((1, 256),)),
        "mixing": scatter_about(arg_keys[4], (H, H), H ** -0.5, 0.375),
        "input_weight": scatter_about(arg_keys[5], (H, F), F ** -0.5, 0.5),
        "tiles": scatter_about(arg_keys[6], (N_ROW, N_COL, CAP, TILE, TILE), (N // 4) ** -0.5, 0.0625, ((0, 16), (1, 16))),
        "tile_rows": draw_tile_rows(jax.random.fold_in(arg_keys[10], 71), 0),
        "tile_cols": draw_tile_cols(jax.random.fold_in(arg_keys[10], 71), 0),
        "live_tiles": draw_live_tiles(jax.random.fold_in(arg_keys[10], 71), 0),
    }


def round_half(values):
    narrow = values.astype(jnp.bfloat16)
    narrow = lax.optimization_barrier(narrow)
    return narrow.astype(jnp.float32)


def reference(state, adjoint, features, cotangent, mixing, input_weight, tiles, tile_rows, tile_cols, live_tiles):
    hidden = state.shape[0]
    width_rows = BR * TILE
    width_cols = BC * TILE
    state_wide = state.astype(jnp.float32)
    adjoint_wide = adjoint.astype(jnp.float32)

    def device_step(index, carry):
        forward_sum, backward_sum = carry
        index = index.astype(jnp.int32)
        row_index = index // N_COL
        col_index = index % N_COL
        block_tiles = tiles[row_index, col_index].astype(jnp.float32)
        rows_here = tile_rows[row_index, col_index]
        cols_here = tile_cols[row_index, col_index]
        live = (jnp.arange(CAP, dtype=jnp.int32) < live_tiles[row_index, col_index]).astype(jnp.float32)
        row_start = (row_index * width_rows).astype(jnp.int32)
        col_start = (col_index * width_cols).astype(jnp.int32)
        state_part = lax.dynamic_slice_in_dim(state_wide, row_start, width_rows, 1).reshape(hidden, BR, TILE)
        adjoint_part = lax.dynamic_slice_in_dim(adjoint_wide, col_start, width_cols, 1).reshape(hidden, BC, TILE)
        chosen_state = jnp.take(state_part, rows_here, axis=1)
        forward_terms = jnp.einsum("hsk,skn->hsn", chosen_state, block_tiles, precision=lax.Precision.HIGHEST)
        forward_terms = forward_terms * live[None, :, None]
        forward_local = jnp.zeros((hidden, BC, TILE), jnp.float32).at[:, cols_here].add(forward_terms)
        chosen_adjoint = jnp.take(adjoint_part, cols_here, axis=1)
        backward_terms = jnp.einsum("hsn,skn->hsk", chosen_adjoint, block_tiles, precision=lax.Precision.HIGHEST)
        backward_terms = backward_terms * live[None, :, None]
        backward_local = jnp.zeros((hidden, BR, TILE), jnp.float32).at[:, rows_here].add(backward_terms)
        forward_local = round_half(forward_local)
        backward_local = round_half(backward_local)
        forward_old = lax.dynamic_slice_in_dim(forward_sum, col_start, width_cols, 1)
        forward_sum = lax.dynamic_update_slice_in_dim(forward_sum, forward_old + forward_local.reshape(hidden, width_cols), col_start, 1)
        backward_old = lax.dynamic_slice_in_dim(backward_sum, row_start, width_rows, 1)
        backward_sum = lax.dynamic_update_slice_in_dim(backward_sum, backward_old + backward_local.reshape(hidden, width_rows), row_start, 1)
        return forward_sum, backward_sum

    empty = jnp.zeros((hidden, N), jnp.float32)
    forward_sum, backward_sum = lax.fori_loop(0, N_ROW * N_COL, device_step, (empty, empty))
    flow = forward_sum.astype(jnp.bfloat16)
    pre = jnp.dot(mixing, flow, preferred_element_type=jnp.float32) + jnp.dot(input_weight, features, preferred_element_type=jnp.float32)
    new_state = jnp.tanh(pre).astype(jnp.bfloat16)
    back = backward_sum.astype(jnp.bfloat16)
    slope = 1.0 - state_wide * state_wide
    new_adjoint = (slope * (jnp.dot(mixing.T, back, preferred_element_type=jnp.float32) + cotangent.astype(jnp.float32))).astype(jnp.bfloat16)
    return new_state, new_adjoint
```

```python
import functools

import jax
import jax.numpy as jnp
from jax import lax
from jax.experimental import pallas as pl
from jax.experimental.pallas import tpu as pltpu
from jax.sharding import PartitionSpec as P

SIDE = 128
BF16 = jnp.bfloat16
F32 = jnp.float32
COPIES = 72


def slot_table(rows, cols, count, blocks):
    slots = rows.shape[0]
    ids = jnp.arange(slots, dtype=jnp.int32)
    places = rows * blocks + cols
    here = (places[None, :] == jnp.arange(blocks * blocks, dtype=jnp.int32)[:, None]) & (ids < count)[None, :]
    return slots + jnp.sum(jnp.where(here, ids[None, :] - slots, 0), axis=1, dtype=jnp.int32)


def kernel(
    slot_of,
    state_hbm,
    adjoint_hbm,
    features,
    cotangent,
    mixing,
    input_weight,
    tiles_hbm,
    new_state,
    new_adjoint,
    tiles,
    dense,
    states,
    adjoints,
    fpart,
    bpart,
    fhalf_up,
    fhalf_down,
    ffull_up,
    ffull_down,
    fsum,
    fin,
    bcore,
    bhalf_up,
    bhalf_down,
    bfull_up,
    bfull_down,
    bsum,
    bin_,
    local_sems,
    send_sems,
    recv_sems,
):
    row = lax.axis_index("row")
    col = lax.axis_index("col")
    x, zl = row // 4, row % 4
    y, zh, core = col // 4, (col // 2) % 2, col % 2
    slots = tiles_hbm.shape[0]

    def row_of(dx, dz):
        return ((x + dx) % 4) * 4 + (zl + dz) % 4

    def col_of(dy, dh, dk):
        return ((y + dy) % 4) * 4 + ((zh + dh) % 2) * 2 + (core + dk) % 2

    def to_row(dx, dz):
        return {"row": row_of(dx, dz), "col": col}

    def to_col(dy, dh, dk):
        return {"row": row, "col": col_of(dy, dh, dk)}

    partners = [to_col(0, 0, 1), to_col(0, 1, 0), to_col(1, 0, 0), to_col(3, 0, 0)]
    partners += [to_row(1, 0), to_row(3, 0), to_row(0, 1), to_row(0, 2), to_row(0, 3)]
    barrier = pltpu.get_barrier_semaphore()
    for partner in partners:
        pl.semaphore_signal(barrier, inc=1, device_id=partner, device_id_type=pl.DeviceIdType.MESH)

    sent = []
    names = {}

    def number(name):
        return names.setdefault(name, len(names))

    def send(name, src, dst, device):
        n = number(name)
        copy = pltpu.make_async_remote_copy(
            src_ref=src,
            dst_ref=dst,
            send_sem=send_sems.at[n],
            recv_sem=recv_sems.at[n],
            device_id=device,
            device_id_type=pl.DeviceIdType.MESH,
        )
        copy.start()
        sent.append(copy)

    def arrived(name, ref):
        n = number(name)
        pltpu.make_async_remote_copy(
            src_ref=ref,
            dst_ref=ref,
            send_sem=send_sems.at[n],
            recv_sem=recv_sems.at[n],
            device_id=partners[0],
            device_id_type=pl.DeviceIdType.MESH,
        ).wait_recv()

    upper, lower = pl.ds(0, 128), pl.ds(128, 128)

    tile_copy = pltpu.make_async_copy(tiles_hbm, tiles.at[pl.ds(0, slots)], local_sems.at[0])
    state_copy = pltpu.make_async_copy(state_hbm, states.at[col], local_sems.at[1])
    adjoint_copy = pltpu.make_async_copy(adjoint_hbm, adjoints.at[row], local_sems.at[2])
    state_copy.start()
    adjoint_copy.start()
    tile_copy.start()
    tiles[slots] = jnp.zeros((SIDE, SIDE), BF16)
    pl.semaphore_wait(barrier, len(partners))

    send("s_z", state_hbm, states.at[col], to_col(0, 1, 0))
    for d in (1, 3, 2):
        send(f"a_z{d}", adjoint_hbm, adjoints.at[row], to_row(0, d))
    send("s_up0", state_hbm, states.at[col], to_col(1, 0, 0))
    send("s_dn0", state_hbm, states.at[col], to_col(3, 0, 0))
    send("a_up0", adjoint_hbm, adjoints.at[row], to_row(1, 0))
    send("a_dn0", adjoint_hbm, adjoints.at[row], to_row(3, 0))
    send("s_k00", state_hbm, states.at[col], to_col(0, 0, 1))

    tile_copy.wait()
    blocks = dense.shape[0] // SIDE

    def place(r, carry):
        start = pl.multiple_of(r * SIDE, SIDE)
        for c in range(blocks):
            dense[pl.ds(start, SIDE), c * SIDE : (c + 1) * SIDE] = tiles[slot_of[r * blocks + c]]
        return carry

    lax.fori_loop(0, blocks, place, 0)

    block = states.at[col_of(0, 1, 0)]
    arrived("s_z", block)
    send("s_up1", block, block, to_col(1, 0, 0))
    send("s_dn1", block, block, to_col(3, 0, 0))
    send("s_k01", block, block, to_col(0, 0, 1))
    for d in (1, 3, 2):
        block = adjoints.at[row_of(0, 4 - d)]
        arrived(f"a_z{d}", block)
        send(f"a_up{d}", block, block, to_row(1, 0))
        send(f"a_dn{d}", block, block, to_row(3, 0))

    for h in (0, 1):
        block = states.at[col_of(3, h, 0)]
        arrived(f"s_up{h}", block)
        send(f"s_far_up{h}", block.at[upper], block.at[upper], to_col(1, 0, 0))
        send(f"s_k1{h}", block, block, to_col(0, 0, 1))
        block = states.at[col_of(1, h, 0)]
        arrived(f"s_dn{h}", block)
        send(f"s_far_dn{h}", block.at[lower], block.at[lower], to_col(3, 0, 0))
        send(f"s_k3{h}", block, block, to_col(0, 0, 1))
    for d in (0, 1, 3, 2):
        block = adjoints.at[row_of(3, 4 - d)]
        arrived(f"a_up{d}", block)
        send(f"a_far_up{d}", block.at[upper], block.at[upper], to_row(1, 0))
        block = adjoints.at[row_of(1, 4 - d)]
        arrived(f"a_dn{d}", block)
        send(f"a_far_dn{d}", block.at[lower], block.at[lower], to_row(3, 0))
    for h in (0, 1):
        block = states.at[col_of(2, h, 0)]
        arrived(f"s_far_up{h}", block.at[upper])
        arrived(f"s_far_dn{h}", block.at[lower])
        send(f"s_k2{h}", block, block, to_col(0, 0, 1))
    for h in (0, 1):
        for dy in range(4):
            arrived(f"s_k{dy}{h}", states.at[col_of((4 - dy) % 4 if dy in (1, 3) else dy, h, 1)])
    state_copy.wait()

    def forward(first):
        whole = jnp.concatenate([states[i] for i in range(blocks)], axis=1)
        start = pl.multiple_of(first * SIDE, SIDE)
        product = jnp.dot(whole, dense[:, pl.ds(start, 4 * SIDE)], preferred_element_type=F32)
        for i in range(4):
            fpart[first + i] = product[:, i * SIDE : (i + 1) * SIDE].astype(BF16)

    def fset(dx):
        return fpart.at[pl.ds(((x + dx) % 4) * 4, 4)]

    def forward_turn(i, carry):
        forward(((x + 2 + i) % 4) * 4)
        return carry

    forward(((x + 2) % 4) * 4)
    send("f_half_up", fset(2).at[:, upper], fhalf_up, to_row(1, 0))
    send("f_half_dn", fset(2).at[:, lower], fhalf_down, to_row(3, 0))
    forward(((x + 1) % 4) * 4)
    forward(((x + 3) % 4) * 4)
    arrived("f_half_up", fhalf_up)
    mine = fset(1)
    mine[:, 0:128] = (mine[:, 0:128].astype(F32) + fhalf_up[...].astype(F32)).astype(BF16)
    send("f_full_up", mine, ffull_up, to_row(1, 0))
    arrived("f_half_dn", fhalf_down)
    mine = fset(3)
    mine[:, 128:256] = (mine[:, 128:256].astype(F32) + fhalf_down[...].astype(F32)).astype(BF16)
    send("f_full_dn", mine, ffull_down, to_row(3, 0))
    forward(x * 4)

    for d in (0, 1, 3, 2):
        block = adjoints.at[row_of(2, 4 - d)]
        arrived(f"a_far_up{d}", block.at[upper])
        arrived(f"a_far_dn{d}", block.at[lower])
    adjoint_copy.wait()

    def backward(first):
        whole = jnp.concatenate([adjoints[i] for i in range(blocks)], axis=1)
        start = pl.multiple_of(first * SIDE, SIDE)
        product = lax.dot_general(
            whole, dense[pl.ds(start, 4 * SIDE), :], (((1,), (1,)), ((), ())), preferred_element_type=F32
        )
        for i in range(4):
            bpart[i % 2, first // 2 + i // 2] = product[:, i * SIDE : (i + 1) * SIDE].astype(BF16)

    for dy in (2, 1, 3, 0):
        where = ((y + dy) % 4) * 2
        backward(where * 2)
        send(f"b_k{dy}", bpart.at[1 - core, pl.ds(where, 2)], bcore.at[pl.ds(where, 2)], to_col(0, 0, 1))

    arrived("f_full_up", ffull_up)
    arrived("f_full_dn", ffull_down)
    for d in (1, 3, 2, 0):
        place_ = (zl + d) % 4
        total = fpart[x * 4 + place_].astype(F32) + ffull_up[place_].astype(F32) + ffull_down[place_].astype(F32)
        if d:
            fsum[d - 1] = total.astype(BF16)
            send(f"f_z{d}", fsum.at[d - 1], fin.at[d - 1], to_row(0, d))
        else:
            fsum[3] = total.astype(BF16)

    def over_cores(dy):
        where = ((y + dy) % 4) * 2
        arrived(f"b_k{dy}", bcore.at[pl.ds(where, 2)])
        for i in range(2):
            bcore[where + i] = (bcore[where + i].astype(F32) + bpart[core, where + i].astype(F32)).astype(BF16)
        return bcore.at[pl.ds(where, 2)]

    far = over_cores(2)
    send("b_half_up", far.at[:, upper], bhalf_up, to_col(1, 0, 0))
    send("b_half_dn", far.at[:, lower], bhalf_down, to_col(3, 0, 0))
    near = over_cores(1)
    arrived("b_half_up", bhalf_up)
    near[:, 0:128] = (near[:, 0:128].astype(F32) + bhalf_up[...].astype(F32)).astype(BF16)
    send("b_full_up", near, bfull_up, to_col(1, 0, 0))
    near = over_cores(3)
    arrived("b_half_dn", bhalf_down)
    near[:, 128:256] = (near[:, 128:256].astype(F32) + bhalf_down[...].astype(F32)).astype(BF16)
    send("b_full_dn", near, bfull_down, to_col(3, 0, 0))
    over_cores(0)
    arrived("b_full_up", bfull_up)
    arrived("b_full_dn", bfull_down)
    for h in (1, 0):
        place_ = (zh + h) % 2
        total = bcore[y * 2 + place_].astype(F32) + bfull_up[place_].astype(F32) + bfull_down[place_].astype(F32)
        bsum[h] = total.astype(BF16)
        if h:
            send("b_z", bsum.at[1], bin_, to_col(0, 1, 0))

    total = fsum[3].astype(F32)
    for d in (1, 2, 3):
        arrived(f"f_z{d}", fin.at[d - 1])
        total += fin[d - 1].astype(F32)
    flow = total.astype(BF16)
    pre = jnp.dot(mixing[...], flow, preferred_element_type=F32)
    pre += jnp.dot(input_weight[...], features[...], preferred_element_type=F32)
    new_state[...] = jnp.tanh(pre).astype(BF16)
    arrived("b_z", bin_)
    back = (bsum[0].astype(F32) + bin_[...].astype(F32)).astype(BF16)
    pulled = lax.dot_general(mixing[...], back, (((0,), (0,)), ((), ())), preferred_element_type=F32)
    own = states[col].astype(F32)
    new_adjoint[...] = ((1.0 - own * own) * (pulled + cotangent[...].astype(F32))).astype(BF16)

    for copy in sent:
        copy.wait_send()
    assert len(names) <= COPIES


def per_device(state, adjoint, features, cotangent, mixing, input_weight, tiles, tile_rows, tile_cols, live_tiles):
    blocks = lax.axis_size("col")
    slab = tiles[0, 0]
    slots = slab.shape[0]
    hidden, nodes = state.shape
    table = slot_table(tile_rows[0, 0], tile_cols[0, 0], live_tiles[0, 0], blocks)
    vmem = pl.BlockSpec(memory_space=pltpu.VMEM)
    anywhere = pl.BlockSpec(memory_space=pl.ANY)
    block = (hidden, nodes)
    half = (hidden // 2, nodes)
    return pl.pallas_call(
        kernel,
        out_shape=(jax.ShapeDtypeStruct(block, BF16), jax.ShapeDtypeStruct(block, BF16)),
        in_specs=[
            pl.BlockSpec(memory_space=pltpu.SMEM),
            anywhere,
            anywhere,
            vmem,
            vmem,
            vmem,
            vmem,
            anywhere,
        ],
        out_specs=(vmem, vmem),
        scratch_shapes=[
            pltpu.VMEM((slots + 1, SIDE, SIDE), BF16),
            pltpu.VMEM((blocks * SIDE, blocks * SIDE), BF16),
            pltpu.VMEM((blocks, *block), BF16),
            pltpu.VMEM((blocks, *block), BF16),
            pltpu.VMEM((blocks, *block), BF16),
            pltpu.VMEM((2, blocks // 2, *block), BF16),
            pltpu.VMEM((4, *half), BF16),
            pltpu.VMEM((4, *half), BF16),
            pltpu.VMEM((4, *block), BF16),
            pltpu.VMEM((4, *block), BF16),
            pltpu.VMEM((4, *block), BF16),
            pltpu.VMEM((3, *block), BF16),
            pltpu.VMEM((blocks // 2, *block), BF16),
            pltpu.VMEM((2, *half), BF16),
            pltpu.VMEM((2, *half), BF16),
            pltpu.VMEM((2, *block), BF16),
            pltpu.VMEM((2, *block), BF16),
            pltpu.VMEM((2, *block), BF16),
            pltpu.VMEM(block, BF16),
            pltpu.SemaphoreType.DMA((3,)),
            pltpu.SemaphoreType.DMA((COPIES,)),
            pltpu.SemaphoreType.DMA((COPIES,)),
        ],
        compiler_params=pltpu.CompilerParams(
            collective_id=0, has_side_effects=True, vmem_limit_bytes=56 * 1024 * 1024
        ),
        name="joint_step",
    )(table, state, adjoint, features, cotangent, mixing, input_weight, slab)


def solution(mesh):
    placed = (
        P(None, ("row", "col")),
        P(None, ("col", "row")),
        P(None, ("col", "row")),
        P(None, ("row", "col")),
        P(),
        P(),
        P("row", "col", None, None, None),
        P("row", "col", None),
        P("row", "col", None),
        P("row", "col"),
    )
    return jax.shard_map(
        per_device,
        mesh=mesh,
        in_specs=placed,
        out_specs=(P(None, ("col", "row")), P(None, ("row", "col"))),
        check_vma=False,
    )
```

```python
import functools

import jax
import jax.numpy as jnp
from jax import lax
from jax.experimental import pallas as pl
from jax.experimental.pallas import tpu as pltpu
from jax.sharding import PartitionSpec as P

SIDE = 128
BF16 = jnp.bfloat16
F32 = jnp.float32
COPIES = 72


def kernel(
    tile_rows,
    tile_cols,
    live_tiles,
    state_hbm,
    adjoint_hbm,
    tiles_hbm,
    flow,
    back,
    tiles,
    dense,
    table,
    slot_of,
    states,
    adjoints,
    fpart,
    fhalf_up,
    fhalf_down,
    ffull_up,
    ffull_down,
    ftotal,
    fsum,
    fin,
    bpart,
    bcore,
    bring,
    btotal,
    bsum,
    bin_,
    local_sems,
    send_sems,
    recv_sems,
):
    row = lax.axis_index("row")
    col = lax.axis_index("col")
    x, zl = row // 4, row % 4
    y, zh, core = col // 4, (col // 2) % 2, col % 2
    slots = tiles_hbm.shape[0]
    blocks = dense.shape[0] // SIDE

    def row_of(dx, dz):
        return ((x + dx) % 4) * 4 + (zl + dz) % 4

    def col_of(dy, dh, dk):
        return ((y + dy) % 4) * 4 + ((zh + dh) % 2) * 2 + (core + dk) % 2

    def to_row(dx, dz):
        return {"row": row_of(dx, dz), "col": col}

    def to_col(dy, dh, dk):
        return {"row": row, "col": col_of(dy, dh, dk)}

    partners = [to_col(0, 1, 0), to_row(0, 1), to_row(0, 2), to_row(0, 3)]
    partners += [to_col(2, 0, 0), to_col(1, 0, 0), to_col(3, 0, 0), to_row(1, 0), to_row(3, 0), to_col(0, 0, 1)]
    barrier = pltpu.get_barrier_semaphore()
    for partner in partners:
        pl.semaphore_signal(barrier, inc=1, device_id=partner, device_id_type=pl.DeviceIdType.MESH)

    end = (zl == 0) | (zl == 3)
    near = [
        jnp.where(zl == 0, 3, 1),
        jnp.where(end, 2, 3),
        jnp.where(zl == 0, 1, jnp.where(zl == 3, 3, 2)),
    ]

    sent = []
    names = {}
    used = [0]

    def number(name, count=1):
        if name not in names:
            names[name] = used[0]
            used[0] += count
        return names[name]

    def send(name, src, dst, device, which=0, count=1):
        n = number(name, count) + which
        copy = pltpu.make_async_remote_copy(
            src_ref=src,
            dst_ref=dst,
            send_sem=send_sems.at[n],
            recv_sem=recv_sems.at[n],
            device_id=device,
            device_id_type=pl.DeviceIdType.MESH,
        )
        copy.start()
        sent.append(copy)

    def arrived(name, ref, which=0):
        n = names[name] + which
        pltpu.make_async_remote_copy(
            src_ref=ref,
            dst_ref=ref,
            send_sem=send_sems.at[n],
            recv_sem=recv_sems.at[n],
            device_id=partners[0],
            device_id_type=pl.DeviceIdType.MESH,
        ).wait_recv()

    upper, lower = pl.ds(0, 128), pl.ds(128, 128)

    state_copy = pltpu.make_async_copy(state_hbm, states.at[col], local_sems.at[0])
    adjoint_copy = pltpu.make_async_copy(adjoint_hbm, adjoints.at[row], local_sems.at[1])
    tile_copy = pltpu.make_async_copy(tiles_hbm, tiles.at[pl.ds(0, slots)], local_sems.at[2])
    state_copy.start()
    adjoint_copy.start()
    tile_copy.start()
    tiles[slots] = jnp.zeros((SIDE, SIDE), BF16)

    places = tile_rows[...] * blocks + tile_cols[...]
    across = lax.broadcasted_iota(jnp.int32, (slots, slots), 1)
    down = lax.broadcasted_iota(jnp.int32, (slots, slots), 0)
    places = jnp.sum(jnp.where(across == down, jnp.broadcast_to(places, (slots, slots)), 0), axis=1, keepdims=True)
    ids = lax.broadcasted_iota(jnp.int32, (slots, SIDE), 0)
    for part in range(blocks * blocks // SIDE):
        here = (places == lax.broadcasted_iota(jnp.int32, (slots, SIDE), 1) + part * SIDE) & (ids < live_tiles[0, 0])
        found = jnp.sum(jnp.where(here, ids - slots, 0), axis=0, keepdims=True)
        table[part : part + 1] = found + slots
    table_copy = pltpu.make_async_copy(table, slot_of, local_sems.at[3])
    table_copy.start()
    state_copy.wait()
    adjoint_copy.wait()
    pl.semaphore_wait(barrier, len(partners))

    own_state, own_adjoint = states.at[col], adjoints.at[row]
    send("s_z", own_state, own_state, to_col(0, 1, 0))
    send("a_z", own_adjoint, own_adjoint, to_row(0, 4 - near[0]), 4 - near[0], 4)
    send("a_up0", own_adjoint, own_adjoint, to_row(1, 0))
    send("a_dn0", own_adjoint, own_adjoint, to_row(3, 0))
    send("a_z", own_adjoint, own_adjoint, to_row(0, 4 - near[1]), 4 - near[1], 4)
    send("a_z", own_adjoint, own_adjoint, to_row(0, 4 - near[2]), 4 - near[2], 4)
    for dy in (2, 1, 3):
        send(f"s_y{dy}0", own_state, own_state, to_col(dy, 0, 0))
    send("s_k00", own_state, own_state, to_col(0, 0, 1))

    tile_copy.wait()
    table_copy.wait()

    def place(r, carry):
        start = pl.multiple_of(r * SIDE, SIDE)
        for c in range(blocks):
            n = r * blocks + c
            dense[pl.ds(start, SIDE), c * SIDE : (c + 1) * SIDE] = tiles[slot_of[n // SIDE, n % SIDE]]
        return carry

    lax.fori_loop(0, blocks, place, 0)

    def adjoint_onward(i):
        block = adjoints.at[row_of(0, 4 - near[i])]
        arrived("a_z", block, near[i])
        send(f"a_up{i + 1}", block, block, to_row(1, 0))
        send(f"a_dn{i + 1}", block, block, to_row(3, 0))

    def adjoint_far(i):
        dz = 4 - near[i - 1] if i else 0
        block = adjoints.at[row_of(3, dz)]
        arrived(f"a_up{i}", block)
        send(f"a_far_up{i}", block.at[upper], block.at[upper], to_row(1, 0))
        block = adjoints.at[row_of(1, dz)]
        arrived(f"a_dn{i}", block)
        send(f"a_far_dn{i}", block.at[lower], block.at[lower], to_row(3, 0))

    adjoint_onward(0)
    adjoint_far(0)
    block = states.at[col_of(0, 1, 0)]
    arrived("s_z", block)
    for dy in (2, 1, 3):
        send(f"s_y{dy}1", block, block, to_col(dy, 0, 0))
    send("s_k01", block, block, to_col(0, 0, 1))
    adjoint_onward(1)
    adjoint_far(1)
    for dy in (1, 3, 2):
        block = states.at[col_of(4 - dy, 0, 0)]
        arrived(f"s_y{dy}0", block)
        send(f"s_k{dy}0", block, block, to_col(0, 0, 1))
    adjoint_onward(2)
    adjoint_far(2)
    for dy in (1, 3, 2):
        block = states.at[col_of(4 - dy, 1, 0)]
        arrived(f"s_y{dy}1", block)
        send(f"s_k{dy}1", block, block, to_col(0, 0, 1))
    adjoint_far(3)
    for h in (0, 1):
        for dy in (0, 1, 3, 2):
            arrived(f"s_k{dy}{h}", states.at[col_of(4 - dy, h, 1)])

    def forward(dx):
        first = ((x + dx) % 4) * 4
        whole = jnp.concatenate([states[i] for i in range(blocks)], axis=1)
        start = pl.multiple_of(first * SIDE, SIDE)
        product = jnp.dot(whole, dense[:, pl.ds(start, 4 * SIDE)], preferred_element_type=F32)
        for i in range(4):
            fpart[first + i] = product[:, i * SIDE : (i + 1) * SIDE].astype(BF16)

    zorder = [4 - near[2], 4 - near[1], 4 - near[0], 0]

    forward(2)
    for i, dz in enumerate(zorder):
        block = fpart.at[row_of(2, dz)]
        send(f"f_half_up{i}", block.at[upper], fhalf_up.at[i], to_row(1, 0))
        send(f"f_half_dn{i}", block.at[lower], fhalf_down.at[i], to_row(3, 0))
    forward(1)
    forward(3)
    for i, dz in enumerate(zorder):
        block = fpart.at[row_of(1, dz)]
        arrived(f"f_half_up{i}", fhalf_up.at[i])
        block[0:128] = (block[0:128].astype(F32) + fhalf_up[i].astype(F32)).astype(BF16)
        send(f"f_full_up{i}", block, ffull_up.at[i], to_row(1, 0))
        block = fpart.at[row_of(3, dz)]
        arrived(f"f_half_dn{i}", fhalf_down.at[i])
        block[128:256] = (block[128:256].astype(F32) + fhalf_down[i].astype(F32)).astype(BF16)
        send(f"f_full_dn{i}", block, ffull_down.at[i], to_row(3, 0))
    forward(0)

    for i in range(4):
        block = adjoints.at[row_of(2, 4 - near[i - 1] if i else 0)]
        arrived(f"a_far_up{i}", block.at[upper])
        arrived(f"a_far_dn{i}", block.at[lower])

    def backward(dy):
        first = ((y + dy) % 4) * 4
        whole = jnp.concatenate([adjoints[i] for i in range(blocks)], axis=1)
        start = pl.multiple_of(first * SIDE, SIDE)
        product = lax.dot_general(
            whole, dense[pl.ds(start, 4 * SIDE), :], (((1,), (1,)), ((), ())), preferred_element_type=F32
        )
        for i in range(4):
            bpart[i % 2, first // 2 + i // 2] = product[:, i * SIDE : (i + 1) * SIDE].astype(BF16)

    for dy in (2, 1, 3, 0):
        backward(dy)
        pair = pl.ds(((y + dy) % 4) * 2, 2)
        send(f"b_k{dy}", bpart.at[1 - core, pair], bcore.at[pair], to_col(0, 0, 1))

    for dy in (2, 1, 3, 0):
        first = ((y + dy) % 4) * 2
        pair = pl.ds(first, 2)
        arrived(f"b_k{dy}", bcore.at[pair])
        if dy:
            for i in range(2):
                bcore[first + i] = (bcore[first + i].astype(F32) + bpart[core, first + i].astype(F32)).astype(BF16)
            send(f"b_y{dy}", bcore.at[pair], bring.at[dy - 1], to_col(dy, 0, 0))

    def forward_sum(i):
        arrived(f"f_full_up{i}", ffull_up.at[i])
        arrived(f"f_full_dn{i}", ffull_down.at[i])
        dz = zorder[i]
        total = fpart[row_of(0, dz)].astype(F32) + ffull_up[i].astype(F32) + ffull_down[i].astype(F32)
        if i < 3:
            fsum[i] = total.astype(BF16)
            send("f_z", fsum.at[i], fin.at[dz - 1], to_row(0, dz), dz, 4)
        else:
            ftotal[...] = total

    forward_sum(0)
    forward_sum(1)
    for dy in (1, 3, 2):
        arrived(f"b_y{dy}", bring.at[dy - 1])
    for h in (1, 0):
        n = (zh + h) % 2
        total = bcore[y * 2 + n].astype(F32) + bpart[core, y * 2 + n].astype(F32)
        for dy in (1, 2, 3):
            total += bring[dy - 1, n].astype(F32)
        if h:
            bsum[...] = total.astype(BF16)
            send("b_z", bsum, bin_, to_col(0, 1, 0))
        else:
            btotal[...] = total
    forward_sum(2)
    forward_sum(3)

    total = ftotal[...]
    for d in (1, 2, 3):
        arrived("f_z", fin.at[d - 1], d)
        total += fin[d - 1].astype(F32)
    flow[...] = total.astype(BF16)
    arrived("b_z", bin_)
    back[...] = (btotal[...] + bin_[...].astype(F32)).astype(BF16)

    for copy in sent:
        copy.wait_send()
    assert used[0] <= COPIES


def per_device(state, adjoint, features, cotangent, mixing, input_weight, tiles, tile_rows, tile_cols, live_tiles):
    blocks = lax.axis_size("col")
    slab = tiles[0, 0]
    slots = slab.shape[0]
    hidden, nodes = state.shape
    vmem = pl.BlockSpec(memory_space=pltpu.VMEM)
    smem = pl.BlockSpec(memory_space=pltpu.SMEM)
    anywhere = pl.BlockSpec(memory_space=pl.ANY)
    block = (hidden, nodes)
    half = (hidden // 2, nodes)
    flow, back = pl.pallas_call(
        kernel,
        out_shape=(jax.ShapeDtypeStruct(block, BF16), jax.ShapeDtypeStruct(block, BF16)),
        in_specs=[vmem, vmem, smem, anywhere, anywhere, anywhere],
        out_specs=(vmem, vmem),
        scratch_shapes=[
            pltpu.VMEM((slots + 1, SIDE, SIDE), BF16),
            pltpu.VMEM((blocks * SIDE, blocks * SIDE), BF16),
            pltpu.VMEM((blocks * blocks // SIDE, SIDE), jnp.int32),
            pltpu.SMEM((blocks * blocks // SIDE, SIDE), jnp.int32),
            pltpu.VMEM((blocks, *block), BF16),
            pltpu.VMEM((blocks, *block), BF16),
            pltpu.VMEM((blocks, *block), BF16),
            pltpu.VMEM((4, *half), BF16),
            pltpu.VMEM((4, *half), BF16),
            pltpu.VMEM((4, *block), BF16),
            pltpu.VMEM((4, *block), BF16),
            pltpu.VMEM(block, F32),
            pltpu.VMEM((3, *block), BF16),
            pltpu.VMEM((3, *block), BF16),
            pltpu.VMEM((2, blocks // 2, *block), BF16),
            pltpu.VMEM((blocks // 2, *block), BF16),
            pltpu.VMEM((3, 2, *block), BF16),
            pltpu.VMEM(block, F32),
            pltpu.VMEM(block, BF16),
            pltpu.VMEM(block, BF16),
            pltpu.SemaphoreType.DMA((4,)),
            pltpu.SemaphoreType.DMA((COPIES,)),
            pltpu.SemaphoreType.DMA((COPIES,)),
        ],
        compiler_params=pltpu.CompilerParams(
            collective_id=0, has_side_effects=True, vmem_limit_bytes=56 * 1024 * 1024
        ),
        name="joint_step",
    )(tile_rows[0], tile_cols[0], live_tiles, state, adjoint, slab)
    pre = jnp.dot(mixing, flow, preferred_element_type=F32)
    pre = pre + jnp.dot(input_weight, features, preferred_element_type=F32)
    new_state = jnp.tanh(pre).astype(BF16)
    pulled = jnp.dot(mixing.T, back, preferred_element_type=F32)
    wide = state.astype(F32)
    new_adjoint = ((1.0 - wide * wide) * (pulled + cotangent.astype(F32))).astype(BF16)
    return new_state, new_adjoint


def solution(mesh):
    placed = (
        P(None, ("row", "col")),
        P(None, ("col", "row")),
        P(None, ("col", "row")),
        P(None, ("row", "col")),
        P(),
        P(),
        P("row", "col", None, None, None),
        P("row", "col", None),
        P("row", "col", None),
        P("row", "col"),
    )
    return jax.shard_map(
        per_device,
        mesh=mesh,
        in_specs=placed,
        out_specs=(P(None, ("col", "row")), P(None, ("row", "col"))),
        check_vma=False,
    )
```

```python
import functools

import jax
import jax.numpy as jnp
from jax import lax
from jax.experimental import pallas as pl
from jax.experimental.pallas import tpu as pltpu
from jax.sharding import PartitionSpec as P

SIDE = 128
BF16 = jnp.bfloat16
F32 = jnp.float32
COPIES = 72


def kernel(
    state_hbm,
    adjoint_hbm,
    tiles_hbm,
    tile_rows_hbm,
    tile_cols_hbm,
    live_tiles_hbm,
    features_hbm,
    cotangent_hbm,
    mixing_hbm,
    input_weight_hbm,
    result,
    tile_rows,
    tile_cols,
    live_tiles,
    features,
    cotangent,
    mixing,
    input_weight,
    tiles,
    dense,
    table,
    slot_of,
    states,
    adjoints,
    fpart,
    fhalf_up,
    fhalf_down,
    ffull_up,
    ffull_down,
    ftotal,
    fsum,
    fin,
    bpart,
    bcore,
    bring,
    btotal,
    bsum,
    bin_,
    local_sems,
    send_sems,
    recv_sems,
):
    row = lax.axis_index("row")
    col = lax.axis_index("col")
    x, zl = row // 4, row % 4
    y, zh, core = col // 4, (col // 2) % 2, col % 2
    slots = tiles_hbm.shape[0]
    blocks = dense.shape[0] // SIDE

    def row_of(dx, dz):
        return ((x + dx) % 4) * 4 + (zl + dz) % 4

    def col_of(dy, dh, dk):
        return ((y + dy) % 4) * 4 + ((zh + dh) % 2) * 2 + (core + dk) % 2

    def to_row(dx, dz):
        return {"row": row_of(dx, dz), "col": col}

    def to_col(dy, dh, dk):
        return {"row": row, "col": col_of(dy, dh, dk)}

    partners = [to_col(0, 1, 0), to_row(0, 1), to_row(0, 2), to_row(0, 3)]
    partners += [to_col(2, 0, 0), to_col(1, 0, 0), to_col(3, 0, 0), to_row(1, 0), to_row(3, 0), to_col(0, 0, 1)]
    barrier = pltpu.get_barrier_semaphore()
    for partner in partners:
        pl.semaphore_signal(barrier, inc=1, device_id=partner, device_id_type=pl.DeviceIdType.MESH)

    end = (zl == 0) | (zl == 3)
    near = [
        jnp.where(zl == 0, 3, 1),
        jnp.where(end, 2, 3),
        jnp.where(zl == 0, 1, jnp.where(zl == 3, 3, 2)),
    ]

    sent = []
    names = {}
    used = [0]

    def number(name, count=1):
        if name not in names:
            names[name] = used[0]
            used[0] += count
        return names[name]

    def send(name, src, dst, device, which=0, count=1):
        n = number(name, count) + which
        copy = pltpu.make_async_remote_copy(
            src_ref=src,
            dst_ref=dst,
            send_sem=send_sems.at[n],
            recv_sem=recv_sems.at[n],
            device_id=device,
            device_id_type=pl.DeviceIdType.MESH,
        )
        copy.start()
        sent.append(copy)

    def arrived(name, ref, which=0):
        n = names[name] + which
        pltpu.make_async_remote_copy(
            src_ref=ref,
            dst_ref=ref,
            send_sem=send_sems.at[n],
            recv_sem=recv_sems.at[n],
            device_id=partners[0],
            device_id_type=pl.DeviceIdType.MESH,
        ).wait_recv()

    upper, lower = pl.ds(0, 128), pl.ds(128, 128)

    def fetch(src, dst, n):
        copy = pltpu.make_async_copy(src, dst, local_sems.at[n])
        copy.start()
        return copy

    index_copies = [
        fetch(tile_rows_hbm, tile_rows, 4),
        fetch(tile_cols_hbm, tile_cols, 5),
        fetch(live_tiles_hbm, live_tiles, 6),
    ]
    state_copy = fetch(state_hbm, states.at[col], 0)
    adjoint_copy = fetch(adjoint_hbm, adjoints.at[row], 1)
    tile_copy = fetch(tiles_hbm, tiles.at[pl.ds(0, slots)], 2)
    late_copies = [
        fetch(features_hbm, features, 7),
        fetch(cotangent_hbm, cotangent, 8),
        fetch(mixing_hbm, mixing, 9),
        fetch(input_weight_hbm, input_weight, 10),
    ]
    tiles[slots] = jnp.zeros((SIDE, SIDE), BF16)

    for copy in index_copies:
        copy.wait()

    places = tile_rows[...] * blocks + tile_cols[...]
    across = lax.broadcasted_iota(jnp.int32, (slots, slots), 1)
    down = lax.broadcasted_iota(jnp.int32, (slots, slots), 0)
    places = jnp.sum(jnp.where(across == down, jnp.broadcast_to(places, (slots, slots)), 0), axis=1, keepdims=True)
    ids = lax.broadcasted_iota(jnp.int32, (slots, SIDE), 0)
    for part in range(blocks * blocks // SIDE):
        here = (places == lax.broadcasted_iota(jnp.int32, (slots, SIDE), 1) + part * SIDE) & (ids < live_tiles[0, 0])
        found = jnp.sum(jnp.where(here, ids - slots, 0), axis=0, keepdims=True)
        table[part : part + 1] = found + slots
    table_copy = pltpu.make_async_copy(table, slot_of, local_sems.at[3])
    table_copy.start()
    state_copy.wait()
    adjoint_copy.wait()
    pl.semaphore_wait(barrier, len(partners))

    own_state, own_adjoint = states.at[col], adjoints.at[row]
    send("s_z", own_state, own_state, to_col(0, 1, 0))
    send("a_z", own_adjoint, own_adjoint, to_row(0, 4 - near[0]), 4 - near[0], 4)
    send("a_up0", own_adjoint, own_adjoint, to_row(1, 0))
    send("a_dn0", own_adjoint, own_adjoint, to_row(3, 0))
    send("a_z", own_adjoint, own_adjoint, to_row(0, 4 - near[1]), 4 - near[1], 4)
    send("a_z", own_adjoint, own_adjoint, to_row(0, 4 - near[2]), 4 - near[2], 4)
    for dy in (2, 1, 3):
        send(f"s_y{dy}0", own_state, own_state, to_col(dy, 0, 0))
    send("s_k00", own_state, own_state, to_col(0, 0, 1))

    tile_copy.wait()
    table_copy.wait()

    def place(r, carry):
        start = pl.multiple_of(r * SIDE, SIDE)
        for c in range(blocks):
            n = r * blocks + c
            dense[pl.ds(start, SIDE), c * SIDE : (c + 1) * SIDE] = tiles[slot_of[n // SIDE, n % SIDE]]
        return carry

    lax.fori_loop(0, blocks, place, 0)

    def adjoint_onward(i):
        block = adjoints.at[row_of(0, 4 - near[i])]
        arrived("a_z", block, near[i])
        send(f"a_up{i + 1}", block, block, to_row(1, 0))
        send(f"a_dn{i + 1}", block, block, to_row(3, 0))

    def adjoint_far(i):
        dz = 4 - near[i - 1] if i else 0
        block = adjoints.at[row_of(3, dz)]
        arrived(f"a_up{i}", block)
        send(f"a_far_up{i}", block.at[upper], block.at[upper], to_row(1, 0))
        block = adjoints.at[row_of(1, dz)]
        arrived(f"a_dn{i}", block)
        send(f"a_far_dn{i}", block.at[lower], block.at[lower], to_row(3, 0))

    def states_over(h):
        for dy in (1, 3, 2):
            block = states.at[col_of(4 - dy, h, 0)]
            arrived(f"s_y{dy}{h}", block)
            send(f"s_k{dy}{h}", block, block, to_col(0, 0, 1))

    adjoint_far(0)
    adjoint_onward(0)
    block = states.at[col_of(0, 1, 0)]
    arrived("s_z", block)
    for dy in (2, 1, 3):
        send(f"s_y{dy}1", block, block, to_col(dy, 0, 0))
    send("s_k01", block, block, to_col(0, 0, 1))
    adjoint_onward(1)
    states_over(0)
    adjoint_onward(2)
    adjoint_far(1)
    states_over(1)
    adjoint_far(2)
    for h in (0, 1):
        for dy in (0, 1, 3, 2):
            arrived(f"s_k{dy}{h}", states.at[col_of(4 - dy, h, 1)])

    def forward(dx):
        first = ((x + dx) % 4) * 4
        whole = jnp.concatenate([states[i] for i in range(blocks)], axis=1)
        start = pl.multiple_of(first * SIDE, SIDE)
        product = jnp.dot(whole, dense[:, pl.ds(start, 4 * SIDE)], preferred_element_type=F32)
        for i in range(4):
            fpart[first + i] = product[:, i * SIDE : (i + 1) * SIDE].astype(BF16)

    zorder = [4 - near[2], 4 - near[1], 4 - near[0], 0]

    def backward(dy):
        first = ((y + dy) % 4) * 4
        whole = jnp.concatenate([adjoints[i] for i in range(blocks)], axis=1)
        start = pl.multiple_of(first * SIDE, SIDE)
        product = lax.dot_general(
            whole, dense[pl.ds(start, 4 * SIDE), :], (((1,), (1,)), ((), ())), preferred_element_type=F32
        )
        for i in range(4):
            bpart[i % 2, first // 2 + i // 2] = product[:, i * SIDE : (i + 1) * SIDE].astype(BF16)
        pair = pl.ds(((y + dy) % 4) * 2, 2)
        send(f"b_k{dy}", bpart.at[1 - core, pair], bcore.at[pair], to_col(0, 0, 1))

    def over_cores(dy):
        first = ((y + dy) % 4) * 2
        pair = pl.ds(first, 2)
        arrived(f"b_k{dy}", bcore.at[pair])
        for i in range(2):
            bcore[first + i] = (bcore[first + i].astype(F32) + bpart[core, first + i].astype(F32)).astype(BF16)
        send(f"b_y{dy}", bcore.at[pair], bring.at[dy - 1], to_col(dy, 0, 0))

    def near_sum(i):
        dz = zorder[i]
        block = fpart.at[row_of(1, dz)]
        arrived(f"f_half_up{i}", fhalf_up.at[i])
        block[0:128] = (block[0:128].astype(F32) + fhalf_up[i].astype(F32)).astype(BF16)
        send(f"f_full_up{i}", block, ffull_up.at[i], to_row(1, 0))
        block = fpart.at[row_of(3, dz)]
        arrived(f"f_half_dn{i}", fhalf_down.at[i])
        block[128:256] = (block[128:256].astype(F32) + fhalf_down[i].astype(F32)).astype(BF16)
        send(f"f_full_dn{i}", block, ffull_down.at[i], to_row(3, 0))

    forward(2)
    for i, dz in enumerate(zorder):
        block = fpart.at[row_of(2, dz)]
        send(f"f_half_up{i}", block.at[upper], fhalf_up.at[i], to_row(1, 0))
        send(f"f_half_dn{i}", block.at[lower], fhalf_down.at[i], to_row(3, 0))
    adjoint_far(3)
    forward(1)
    forward(3)
    near_sum(0)
    near_sum(1)

    for i in range(4):
        block = adjoints.at[row_of(2, 4 - near[i - 1] if i else 0)]
        arrived(f"a_far_up{i}", block.at[upper])
        arrived(f"a_far_dn{i}", block.at[lower])
    backward(2)
    near_sum(2)
    near_sum(3)
    backward(1)
    over_cores(2)
    backward(3)
    over_cores(1)
    forward(0)
    over_cores(3)
    backward(0)

    def forward_sum(i):
        arrived(f"f_full_up{i}", ffull_up.at[i])
        arrived(f"f_full_dn{i}", ffull_down.at[i])
        dz = zorder[i]
        total = fpart[row_of(0, dz)].astype(F32) + ffull_up[i].astype(F32) + ffull_down[i].astype(F32)
        if i < 3:
            fsum[i] = total.astype(BF16)
            send("f_z", fsum.at[i], fin.at[dz - 1], to_row(0, dz), dz, 4)
        else:
            ftotal[...] = total

    forward_sum(0)
    forward_sum(1)
    first = y * 2
    arrived("b_k0", bcore.at[pl.ds(first, 2)])
    for dy in (1, 3, 2):
        arrived(f"b_y{dy}", bring.at[dy - 1])
    for h in (1, 0):
        n = (zh + h) % 2
        total = bcore[first + n].astype(F32) + bpart[core, first + n].astype(F32)
        for dy in (1, 2, 3):
            total += bring[dy - 1, n].astype(F32)
        if h:
            bsum[...] = total.astype(BF16)
            send("b_z", bsum, bin_, to_col(0, 1, 0))
        else:
            btotal[...] = total
    forward_sum(2)
    forward_sum(3)

    for copy in late_copies:
        copy.wait()
    fed = jnp.dot(input_weight[...], features[...], preferred_element_type=F32)
    total = ftotal[...]
    for d in (1, 2, 3):
        arrived("f_z", fin.at[d - 1], d)
        total += fin[d - 1].astype(F32)
    result[0] = fed + jnp.dot(mixing[...], total.astype(BF16), preferred_element_type=F32)
    arrived("b_z", bin_)
    back = (btotal[...] + bin_[...].astype(F32)).astype(BF16)
    pulled = lax.dot_general(mixing[...], back, (((0,), (0,)), ((), ())), preferred_element_type=F32)
    result[1] = pulled + cotangent[...].astype(F32)

    for copy in sent:
        copy.wait_send()
    assert used[0] <= COPIES


def per_device(state, adjoint, features, cotangent, mixing, input_weight, tiles, tile_rows, tile_cols, live_tiles):
    blocks = lax.axis_size("col")
    slab = tiles[0, 0]
    slots = slab.shape[0]
    hidden, nodes = state.shape
    vmem = pl.BlockSpec(memory_space=pltpu.VMEM)
    anywhere = pl.BlockSpec(memory_space=pl.ANY)
    block = (hidden, nodes)
    half = (hidden // 2, nodes)
    result = pl.pallas_call(
        kernel,
        out_shape=jax.ShapeDtypeStruct((2, *block), F32),
        in_specs=[anywhere] * 10,
        out_specs=vmem,
        scratch_shapes=[
            pltpu.VMEM((1, slots), jnp.int32),
            pltpu.VMEM((1, slots), jnp.int32),
            pltpu.SMEM((1, 1), jnp.int32),
            pltpu.VMEM(features.shape, BF16),
            pltpu.VMEM(block, BF16),
            pltpu.VMEM(mixing.shape, BF16),
            pltpu.VMEM(input_weight.shape, BF16),
            pltpu.VMEM((slots + 1, SIDE, SIDE), BF16),
            pltpu.VMEM((blocks * SIDE, blocks * SIDE), BF16),
            pltpu.VMEM((blocks * blocks // SIDE, SIDE), jnp.int32),
            pltpu.SMEM((blocks * blocks // SIDE, SIDE), jnp.int32),
            pltpu.VMEM((blocks, *block), BF16),
            pltpu.VMEM((blocks, *block), BF16),
            pltpu.VMEM((blocks, *block), BF16),
            pltpu.VMEM((4, *half), BF16),
            pltpu.VMEM((4, *half), BF16),
            pltpu.VMEM((4, *block), BF16),
            pltpu.VMEM((4, *block), BF16),
            pltpu.VMEM(block, F32),
            pltpu.VMEM((3, *block), BF16),
            pltpu.VMEM((3, *block), BF16),
            pltpu.VMEM((2, blocks // 2, *block), BF16),
            pltpu.VMEM((blocks // 2, *block), BF16),
            pltpu.VMEM((3, 2, *block), BF16),
            pltpu.VMEM(block, F32),
            pltpu.VMEM(block, BF16),
            pltpu.VMEM(block, BF16),
            pltpu.SemaphoreType.DMA((11,)),
            pltpu.SemaphoreType.DMA((COPIES,)),
            pltpu.SemaphoreType.DMA((COPIES,)),
        ],
        compiler_params=pltpu.CompilerParams(
            collective_id=0, has_side_effects=True, vmem_limit_bytes=56 * 1024 * 1024
        ),
        name="joint_step",
    )(
        state,
        adjoint,
        slab,
        tile_rows[0],
        tile_cols[0],
        live_tiles,
        features,
        cotangent,
        mixing,
        input_weight,
    )
    new_state = jnp.tanh(result[0]).astype(BF16)
    wide = state.astype(F32)
    new_adjoint = ((1.0 - wide * wide) * result[1]).astype(BF16)
    return new_state, new_adjoint


def solution(mesh):
    placed = (
        P(None, ("row", "col")),
        P(None, ("col", "row")),
        P(None, ("col", "row")),
        P(None, ("row", "col")),
        P(),
        P(),
        P("row", "col", None, None, None),
        P("row", "col", None),
        P("row", "col", None),
        P("row", "col"),
    )
    return jax.shard_map(
        per_device,
        mesh=mesh,
        in_specs=placed,
        out_specs=(P(None, ("col", "row")), P(None, ("row", "col"))),
        check_vma=False,
    )
```

```python
import functools

import jax
import jax.numpy as jnp
from jax import lax
from jax.experimental import pallas as pl
from jax.experimental.pallas import tpu as pltpu
from jax.sharding import PartitionSpec as P

SIDE = 128
BF16 = jnp.bfloat16
F32 = jnp.float32
COPIES = 96
STRAIGHT = (3,)


def kernel(
    state_hbm,
    adjoint_hbm,
    tiles_hbm,
    tile_rows_hbm,
    tile_cols_hbm,
    live_tiles_hbm,
    features_hbm,
    cotangent_hbm,
    mixing_hbm,
    input_weight_hbm,
    new_state,
    new_adjoint,
    tile_rows,
    tile_cols,
    live_tiles,
    features,
    cotangent,
    mixing,
    input_weight,
    tiles,
    dense,
    table,
    slot_of,
    states,
    adjoints,
    fpart,
    fhalf_up,
    fhalf_down,
    ffull_up,
    ffull_down,
    ftotal,
    fsum,
    fin,
    bpart,
    bcore,
    bring,
    btotal,
    bsum,
    bin_,
    local_sems,
    send_sems,
    recv_sems,
):
    row = lax.axis_index("row")
    col = lax.axis_index("col")
    x, zl = row // 4, row % 4
    y, zh, core = col // 4, (col // 2) % 2, col % 2
    slots = tiles_hbm.shape[0]
    blocks = dense.shape[0] // SIDE

    def row_of(dx, dz):
        return ((x + dx) % 4) * 4 + (zl + dz) % 4

    def col_of(dy, dh, dk):
        return ((y + dy) % 4) * 4 + ((zh + dh) % 2) * 2 + (core + dk) % 2

    def to_row(dx, dz):
        return {"row": row_of(dx, dz), "col": col}

    def to_col(dy, dh, dk):
        return {"row": row, "col": col_of(dy, dh, dk)}

    partners = [to_col(0, 1, 0), to_row(0, 1), to_row(0, 2), to_row(0, 3)]
    partners += [to_row(2, 0), to_col(2, 0, 0), to_col(1, 0, 0), to_col(3, 0, 0), to_row(1, 0), to_row(3, 0), to_col(0, 0, 1)]
    barrier = pltpu.get_barrier_semaphore()
    for partner in partners:
        pl.semaphore_signal(barrier, inc=1, device_id=partner, device_id_type=pl.DeviceIdType.MESH)

    end = (zl == 0) | (zl == 3)
    near = [
        jnp.where(zl == 0, 3, 1),
        jnp.where(end, 2, 3),
        jnp.where(zl == 0, 1, jnp.where(zl == 3, 3, 2)),
    ]

    sent = []
    names = {}
    used = [0]

    def number(name, count=1):
        if name not in names:
            names[name] = used[0]
            used[0] += count
        return names[name]

    def send(name, src, dst, device, which=0, count=1):
        n = number(name, count) + which
        copy = pltpu.make_async_remote_copy(
            src_ref=src,
            dst_ref=dst,
            send_sem=send_sems.at[n],
            recv_sem=recv_sems.at[n],
            device_id=device,
            device_id_type=pl.DeviceIdType.MESH,
        )
        copy.start()
        sent.append(copy)

    def arrived(name, ref, which=0):
        n = names[name] + which
        pltpu.make_async_remote_copy(
            src_ref=ref,
            dst_ref=ref,
            send_sem=send_sems.at[n],
            recv_sem=recv_sems.at[n],
            device_id=partners[0],
            device_id_type=pl.DeviceIdType.MESH,
        ).wait_recv()

    upper, lower = pl.ds(0, 128), pl.ds(128, 128)

    def fetch(src, dst, n):
        copy = pltpu.make_async_copy(src, dst, local_sems.at[n])
        copy.start()
        return copy

    index_copies = [
        fetch(tile_rows_hbm, tile_rows, 4),
        fetch(tile_cols_hbm, tile_cols, 5),
        fetch(live_tiles_hbm, live_tiles, 6),
    ]
    state_copy = fetch(state_hbm, states.at[col], 0)
    adjoint_copy = fetch(adjoint_hbm, adjoints.at[row], 1)
    tile_copy = fetch(tiles_hbm, tiles.at[pl.ds(0, slots)], 2)
    late_copies = [
        fetch(features_hbm, features, 7),
        fetch(cotangent_hbm, cotangent, 8),
        fetch(mixing_hbm, mixing, 9),
        fetch(input_weight_hbm, input_weight, 10),
    ]
    tiles[slots] = jnp.zeros((SIDE, SIDE), BF16)

    for copy in index_copies:
        copy.wait()

    places = tile_rows[...] * blocks + tile_cols[...]
    across = lax.broadcasted_iota(jnp.int32, (slots, slots), 1)
    down = lax.broadcasted_iota(jnp.int32, (slots, slots), 0)
    places = jnp.sum(jnp.where(across == down, jnp.broadcast_to(places, (slots, slots)), 0), axis=1, keepdims=True)
    ids = lax.broadcasted_iota(jnp.int32, (slots, SIDE), 0)
    for part in range(blocks * blocks // SIDE):
        here = (places == lax.broadcasted_iota(jnp.int32, (slots, SIDE), 1) + part * SIDE) & (ids < live_tiles[0, 0])
        found = jnp.sum(jnp.where(here, ids - slots, 0), axis=0, keepdims=True)
        table[part : part + 1] = found + slots
    table_copy = pltpu.make_async_copy(table, slot_of, local_sems.at[3])
    table_copy.start()
    state_copy.wait()
    adjoint_copy.wait()
    pl.semaphore_wait(barrier, len(partners))

    own_state, own_adjoint = states.at[col], adjoints.at[row]
    send("s_z", own_state, own_state, to_col(0, 1, 0))
    send("a_z", own_adjoint, own_adjoint, to_row(0, 4 - near[0]), 4 - near[0], 4)
    send("a_up0", own_adjoint, own_adjoint, to_row(1, 0))
    send("a_dn0", own_adjoint, own_adjoint, to_row(3, 0))
    send("a_z", own_adjoint, own_adjoint, to_row(0, 4 - near[1]), 4 - near[1], 4)
    send("a_z", own_adjoint, own_adjoint, to_row(0, 4 - near[2]), 4 - near[2], 4)
    for dy in (2, 1, 3):
        send(f"s_y{dy}0", own_state, own_state, to_col(dy, 0, 0))
    send("s_k00", own_state, own_state, to_col(0, 0, 1))

    tile_copy.wait()
    table_copy.wait()

    def place(r, carry):
        start = pl.multiple_of(r * SIDE, SIDE)
        for c in range(blocks):
            n = r * blocks + c
            dense[pl.ds(start, SIDE), c * SIDE : (c + 1) * SIDE] = tiles[slot_of[n // SIDE, n % SIDE]]
        return carry

    lax.fori_loop(0, blocks, place, 0)

    def adjoint_onward(i):
        block = adjoints.at[row_of(0, 4 - near[i])]
        arrived("a_z", block, near[i])
        if i + 1 in STRAIGHT:
            send(f"a_x2{i + 1}", block, block, to_row(2, 0))
        send(f"a_up{i + 1}", block, block, to_row(1, 0))
        send(f"a_dn{i + 1}", block, block, to_row(3, 0))

    def adjoint_far(i):
        dz = 4 - near[i - 1] if i else 0
        block = adjoints.at[row_of(3, dz)]
        arrived(f"a_up{i}", block)
        if i in STRAIGHT:
            arrived(f"a_dn{i}", adjoints.at[row_of(1, dz)])
            return
        send(f"a_far_up{i}", block.at[upper], block.at[upper], to_row(1, 0))
        block = adjoints.at[row_of(1, dz)]
        arrived(f"a_dn{i}", block)
        send(f"a_far_dn{i}", block.at[lower], block.at[lower], to_row(3, 0))

    def states_over(h):
        for dy in (1, 3, 2):
            block = states.at[col_of(4 - dy, h, 0)]
            arrived(f"s_y{dy}{h}", block)
            send(f"s_k{dy}{h}", block, block, to_col(0, 0, 1))

    adjoint_onward(0)
    adjoint_far(0)
    block = states.at[col_of(0, 1, 0)]
    arrived("s_z", block)
    for dy in (2, 1, 3):
        send(f"s_y{dy}1", block, block, to_col(dy, 0, 0))
    send("s_k01", block, block, to_col(0, 0, 1))
    adjoint_onward(1)
    states_over(0)
    adjoint_onward(2)
    adjoint_far(1)
    adjoint_far(2)
    adjoint_far(3)

    def forward(dx):
        first = ((x + dx) % 4) * 4
        whole = jnp.concatenate([states[i] for i in range(blocks)], axis=1)
        start = pl.multiple_of(first * SIDE, SIDE)
        product = jnp.dot(whole, dense[:, pl.ds(start, 4 * SIDE)], preferred_element_type=F32)
        for i in range(4):
            fpart[first + i] = product[:, i * SIDE : (i + 1) * SIDE].astype(BF16)

    zorder = [4 - near[2], 4 - near[1], 4 - near[0], 0]

    def backward(dys, h):
        half_of = (zh + h) % 2
        firsts = [((y + dy) % 4) * 4 + half_of * 2 for dy in dys]
        whole = jnp.concatenate([adjoints[i] for i in range(blocks)], axis=1)
        lines = [dense[pl.ds(pl.multiple_of(first * SIDE, 2 * SIDE), 2 * SIDE), :] for first in firsts]
        product = lax.dot_general(
            whole, jnp.concatenate(lines, axis=0), (((1,), (1,)), ((), ())), preferred_element_type=F32
        )
        for i, dy in enumerate(dys):
            slot = firsts[i] // 2
            for k in range(2):
                part = product[:, (2 * i + k) * SIDE : (2 * i + k + 1) * SIDE]
                bpart[k, slot] = part.astype(BF16)
            send(f"b_k{dy}{h}", bpart.at[1 - core, slot], bcore.at[slot], to_col(0, 0, 1))

    def over_cores(dy, h):
        slot = ((y + dy) % 4) * 2 + (zh + h) % 2
        arrived(f"b_k{dy}{h}", bcore.at[slot])
        total = bcore[slot].astype(F32) + bpart[core, slot].astype(F32)
        if dy:
            bcore[slot] = total.astype(BF16)
            send(f"b_y{dy}{h}", bcore.at[slot], bring.at[dy - 1, h], to_col(dy, 0, 0))
        else:
            btotal[h] = total

    def ring_sum(h):
        total = btotal[h]
        for dy in (1, 3, 2):
            arrived(f"b_y{dy}{h}", bring.at[dy - 1, h])
            total += bring[dy - 1, h].astype(F32)
        if h:
            bsum[...] = total.astype(BF16)
            send("b_z", bsum, bin_, to_col(0, 1, 0))
        else:
            btotal[0] = total

    def near_sum(i):
        dz = zorder[i]
        block = fpart.at[row_of(1, dz)]
        arrived(f"f_half_up{i}", fhalf_up.at[i])
        block[0:128] = (block[0:128].astype(F32) + fhalf_up[i].astype(F32)).astype(BF16)
        send(f"f_full_up{i}", block, ffull_up.at[i], to_row(1, 0))
        block = fpart.at[row_of(3, dz)]
        arrived(f"f_half_dn{i}", fhalf_down.at[i])
        block[128:256] = (block[128:256].astype(F32) + fhalf_down[i].astype(F32)).astype(BF16)
        send(f"f_full_dn{i}", block, ffull_down.at[i], to_row(3, 0))

    states_over(1)
    for h in (0, 1):
        for dy in (0, 1, 3, 2):
            arrived(f"s_k{dy}{h}", states.at[col_of(4 - dy, h, 1)])
    forward(2)
    for i, dz in enumerate(zorder):
        block = fpart.at[row_of(2, dz)]
        send(f"f_half_up{i}", block.at[upper], fhalf_up.at[i], to_row(1, 0))
        send(f"f_half_dn{i}", block.at[lower], fhalf_down.at[i], to_row(3, 0))
    for i in range(4):
        block = adjoints.at[row_of(2, 4 - near[i - 1] if i else 0)]
        if i in STRAIGHT:
            arrived(f"a_x2{i}", block)
        else:
            arrived(f"a_far_up{i}", block.at[upper])
            arrived(f"a_far_dn{i}", block.at[lower])
    backward((2, 1), 1)
    backward((3, 0), 1)
    over_cores(2, 1)
    over_cores(1, 1)
    forward(1)
    forward(3)
    over_cores(3, 1)
    over_cores(0, 1)
    near_sum(0)
    near_sum(1)
    backward((2, 1), 0)
    near_sum(2)
    near_sum(3)
    backward((3, 0), 0)
    over_cores(2, 0)
    over_cores(1, 0)
    over_cores(3, 0)
    over_cores(0, 0)
    ring_sum(1)
    forward(0)

    def forward_sum(i):
        arrived(f"f_full_up{i}", ffull_up.at[i])
        arrived(f"f_full_dn{i}", ffull_down.at[i])
        dz = zorder[i]
        total = fpart[row_of(0, dz)].astype(F32) + ffull_up[i].astype(F32) + ffull_down[i].astype(F32)
        if i < 3:
            fsum[i] = total.astype(BF16)
            send("f_z", fsum.at[i], fin.at[dz - 1], to_row(0, dz), dz, 4)
        else:
            ftotal[...] = total

    for i in range(4):
        forward_sum(i)
    ring_sum(0)

    for copy in late_copies:
        copy.wait()
    fed = jnp.dot(input_weight[...], features[...], preferred_element_type=F32)
    total = ftotal[...]
    for d in (1, 2, 3):
        arrived("f_z", fin.at[d - 1], d)
        total += fin[d - 1].astype(F32)
    pre = fed + jnp.dot(mixing[...], total.astype(BF16), preferred_element_type=F32)
    new_state[...] = jnp.tanh(pre).astype(BF16)
    arrived("b_z", bin_)
    back = (btotal[0] + bin_[...].astype(F32)).astype(BF16)
    pulled = lax.dot_general(mixing[...], back, (((0,), (0,)), ((), ())), preferred_element_type=F32)
    own = states[col].astype(F32)
    new_adjoint[...] = ((1.0 - own * own) * (pulled + cotangent[...].astype(F32))).astype(BF16)

    for copy in sent:
        copy.wait_send()
    assert used[0] <= COPIES


def per_device(state, adjoint, features, cotangent, mixing, input_weight, tiles, tile_rows, tile_cols, live_tiles):
    blocks = lax.axis_size("col")
    slab = tiles[0, 0]
    slots = slab.shape[0]
    hidden, nodes = state.shape
    vmem = pl.BlockSpec(memory_space=pltpu.VMEM)
    anywhere = pl.BlockSpec(memory_space=pltpu.HBM)
    block = (hidden, nodes)
    half = (hidden // 2, nodes)
    return pl.pallas_call(
        kernel,
        out_shape=(jax.ShapeDtypeStruct(block, BF16), jax.ShapeDtypeStruct(block, BF16)),
        in_specs=[anywhere] * 10,
        out_specs=(vmem, vmem),
        scratch_shapes=[
            pltpu.VMEM((1, slots), jnp.int32),
            pltpu.VMEM((1, slots), jnp.int32),
            pltpu.SMEM((1, 1), jnp.int32),
            pltpu.VMEM(features.shape, BF16),
            pltpu.VMEM(block, BF16),
            pltpu.VMEM(mixing.shape, BF16),
            pltpu.VMEM(input_weight.shape, BF16),
            pltpu.VMEM((slots + 1, SIDE, SIDE), BF16),
            pltpu.VMEM((blocks * SIDE, blocks * SIDE), BF16),
            pltpu.VMEM((blocks * blocks // SIDE, SIDE), jnp.int32),
            pltpu.SMEM((blocks * blocks // SIDE, SIDE), jnp.int32),
            pltpu.VMEM((blocks, *block), BF16),
            pltpu.VMEM((blocks, *block), BF16),
            pltpu.VMEM((blocks, *block), BF16),
            pltpu.VMEM((4, *half), BF16),
            pltpu.VMEM((4, *half), BF16),
            pltpu.VMEM((4, *block), BF16),
            pltpu.VMEM((4, *block), BF16),
            pltpu.VMEM(block, F32),
            pltpu.VMEM((3, *block), BF16),
            pltpu.VMEM((3, *block), BF16),
            pltpu.VMEM((2, blocks // 2, *block), BF16),
            pltpu.VMEM((blocks // 2, *block), BF16),
            pltpu.VMEM((3, 2, *block), BF16),
            pltpu.VMEM((2, *block), F32),
            pltpu.VMEM(block, BF16),
            pltpu.VMEM(block, BF16),
            pltpu.SemaphoreType.DMA((11,)),
            pltpu.SemaphoreType.DMA((COPIES,)),
            pltpu.SemaphoreType.DMA((COPIES,)),
        ],
        compiler_params=pltpu.CompilerParams(
            collective_id=0, has_side_effects=True, vmem_limit_bytes=26 * 1024 * 1024
        ),
        name="joint_step",
    )(
        *(
            a if a is live_tiles else pltpu.with_memory_space_constraint(a, pltpu.HBM)
            for a in (
                state,
                adjoint,
                slab,
                tile_rows[0],
                tile_cols[0],
                live_tiles,
                features,
                cotangent,
                mixing,
                input_weight,
            )
        )
    )

def solution(mesh):
    placed = (
        P(None, ("row", "col")),
        P(None, ("col", "row")),
        P(None, ("col", "row")),
        P(None, ("row", "col")),
        P(),
        P(),
        P("row", "col", None, None, None),
        P("row", "col", None),
        P("row", "col", None),
        P("row", "col"),
    )
    return jax.shard_map(
        per_device,
        mesh=mesh,
        in_specs=placed,
        out_specs=(P(None, ("col", "row")), P(None, ("row", "col"))),
        check_vma=False,
    )
```

```python
import functools

import jax
import jax.numpy as jnp
from jax import lax
from jax.experimental import pallas as pl
from jax.experimental.pallas import tpu as pltpu
from jax.sharding import PartitionSpec as P

SIDE = 128
BF16 = jnp.bfloat16
F32 = jnp.float32
COPIES = 96
STRAIGHT = (3,)


def kernel(
    state_hbm,
    adjoint_hbm,
    tiles_hbm,
    tile_rows_hbm,
    tile_cols_hbm,
    live_tiles_hbm,
    features_hbm,
    cotangent_hbm,
    mixing_hbm,
    input_weight_hbm,
    new_state,
    new_adjoint,
    tile_rows,
    tile_cols,
    live_tiles,
    features,
    cotangent,
    mixing,
    input_weight,
    tiles,
    dense,
    table,
    slot_of,
    states,
    adjoints,
    fpart,
    fhalf_up,
    fhalf_down,
    ffull_up,
    ffull_down,
    ftotal,
    fsum,
    fin,
    bpart,
    bcore,
    bring,
    btotal,
    bsum,
    bin_,
    local_sems,
    send_sems,
    recv_sems,
):
    row = lax.axis_index("row")
    col = lax.axis_index("col")
    x, zl = row // 4, row % 4
    y, zh, core = col // 4, (col // 2) % 2, col % 2
    slots = tiles_hbm.shape[0]
    blocks = dense.shape[0] // SIDE

    def row_of(dx, dz):
        return ((x + dx) % 4) * 4 + (zl + dz) % 4

    def col_of(dy, dh, dk):
        return ((y + dy) % 4) * 4 + ((zh + dh) % 2) * 2 + (core + dk) % 2

    def to_row(dx, dz):
        return {"row": row_of(dx, dz), "col": col}

    def to_col(dy, dh, dk):
        return {"row": row, "col": col_of(dy, dh, dk)}

    partners = [to_col(0, 1, 0), to_row(0, 1), to_row(0, 2), to_row(0, 3)]
    partners += [to_row(2, 0), to_col(2, 0, 0), to_col(1, 0, 0), to_col(3, 0, 0), to_row(1, 0), to_row(3, 0), to_col(0, 0, 1)]
    barrier = pltpu.get_barrier_semaphore()
    for partner in partners:
        pl.semaphore_signal(barrier, inc=1, device_id=partner, device_id_type=pl.DeviceIdType.MESH)

    end = (zl == 0) | (zl == 3)
    near = [
        jnp.where(zl == 0, 3, 1),
        jnp.where(end, 2, 3),
        jnp.where(zl == 0, 1, jnp.where(zl == 3, 3, 2)),
    ]

    sent = []
    names = {}
    used = [0]

    def number(name, count=1):
        if name not in names:
            names[name] = used[0]
            used[0] += count
        return names[name]

    def send(name, src, dst, device, which=0, count=1):
        n = number(name, count) + which
        copy = pltpu.make_async_remote_copy(
            src_ref=src,
            dst_ref=dst,
            send_sem=send_sems.at[n],
            recv_sem=recv_sems.at[n],
            device_id=device,
            device_id_type=pl.DeviceIdType.MESH,
        )
        copy.start()
        sent.append(copy)

    def arrived(name, ref, which=0):
        n = names[name] + which
        pltpu.make_async_remote_copy(
            src_ref=ref,
            dst_ref=ref,
            send_sem=send_sems.at[n],
            recv_sem=recv_sems.at[n],
            device_id=partners[0],
            device_id_type=pl.DeviceIdType.MESH,
        ).wait_recv()

    upper, lower = pl.ds(0, 128), pl.ds(128, 128)

    def fetch(src, dst, n):
        copy = pltpu.make_async_copy(src, dst, local_sems.at[n])
        copy.start()
        return copy

    index_copies = [
        fetch(tile_rows_hbm, tile_rows, 4),
        fetch(tile_cols_hbm, tile_cols, 5),
        fetch(live_tiles_hbm, live_tiles, 6),
    ]
    state_copy = fetch(state_hbm, states.at[col], 0)
    adjoint_copy = fetch(adjoint_hbm, adjoints.at[row], 1)
    tile_copy = fetch(tiles_hbm, tiles.at[pl.ds(0, slots)], 2)
    late_copies = [
        fetch(features_hbm, features, 7),
        fetch(cotangent_hbm, cotangent, 8),
        fetch(mixing_hbm, mixing, 9),
        fetch(input_weight_hbm, input_weight, 10),
    ]
    tiles[slots] = jnp.zeros((SIDE, SIDE), BF16)

    for copy in index_copies:
        copy.wait()

    places = tile_rows[...] * blocks + tile_cols[...]
    across = lax.broadcasted_iota(jnp.int32, (slots, slots), 1)
    down = lax.broadcasted_iota(jnp.int32, (slots, slots), 0)
    places = jnp.sum(jnp.where(across == down, jnp.broadcast_to(places, (slots, slots)), 0), axis=1, keepdims=True)
    ids = lax.broadcasted_iota(jnp.int32, (slots, SIDE), 0)
    for part in range(blocks * blocks // SIDE):
        here = (places == lax.broadcasted_iota(jnp.int32, (slots, SIDE), 1) + part * SIDE) & (ids < live_tiles[0, 0])
        found = jnp.sum(jnp.where(here, ids - slots, 0), axis=0, keepdims=True)
        table[part : part + 1] = found + slots
    table_copy = pltpu.make_async_copy(table, slot_of, local_sems.at[3])
    table_copy.start()
    state_copy.wait()
    adjoint_copy.wait()
    pl.semaphore_wait(barrier, len(partners))

    own_state, own_adjoint = states.at[col], adjoints.at[row]
    send("s_z", own_state, own_state, to_col(0, 1, 0))
    send("a_z", own_adjoint, own_adjoint, to_row(0, 4 - near[0]), 4 - near[0], 4)
    send("a_z", own_adjoint, own_adjoint, to_row(0, 4 - near[1]), 4 - near[1], 4)
    send("a_z", own_adjoint, own_adjoint, to_row(0, 4 - near[2]), 4 - near[2], 4)
    send("a_up0", own_adjoint, own_adjoint, to_row(1, 0))
    send("a_dn0", own_adjoint, own_adjoint, to_row(3, 0))
    for dy in (2, 1, 3):
        send(f"s_y{dy}0", own_state, own_state, to_col(dy, 0, 0))
    send("s_k00", own_state, own_state, to_col(0, 0, 1))

    tile_copy.wait()
    table_copy.wait()

    def place(r, carry):
        start = pl.multiple_of(r * SIDE, SIDE)
        for c in range(blocks):
            n = r * blocks + c
            dense[pl.ds(start, SIDE), c * SIDE : (c + 1) * SIDE] = tiles[slot_of[n // SIDE, n % SIDE]]
        return carry

    lax.fori_loop(0, blocks, place, 0)

    def adjoint_onward(i):
        block = adjoints.at[row_of(0, 4 - near[i])]
        arrived("a_z", block, near[i])
        if i + 1 in STRAIGHT:
            send(f"a_x2{i + 1}", block, block, to_row(2, 0))
        send(f"a_up{i + 1}", block, block, to_row(1, 0))
        send(f"a_dn{i + 1}", block, block, to_row(3, 0))

    def adjoint_far(i):
        dz = 4 - near[i - 1] if i else 0
        block = adjoints.at[row_of(3, dz)]
        arrived(f"a_up{i}", block)
        if i in STRAIGHT:
            arrived(f"a_dn{i}", adjoints.at[row_of(1, dz)])
            return
        send(f"a_far_up{i}", block.at[upper], block.at[upper], to_row(1, 0))
        block = adjoints.at[row_of(1, dz)]
        arrived(f"a_dn{i}", block)
        send(f"a_far_dn{i}", block.at[lower], block.at[lower], to_row(3, 0))

    def states_over(h):
        for dy in (1, 3, 2):
            block = states.at[col_of(4 - dy, h, 0)]
            arrived(f"s_y{dy}{h}", block)
            send(f"s_k{dy}{h}", block, block, to_col(0, 0, 1))

    def forward(dx):
        first = ((x + dx) % 4) * 4
        whole = jnp.concatenate([states[i] for i in range(blocks)], axis=1)
        start = pl.multiple_of(first * SIDE, SIDE)
        product = jnp.dot(whole, dense[:, pl.ds(start, 4 * SIDE)], preferred_element_type=F32)
        for i in range(4):
            fpart[first + i] = product[:, i * SIDE : (i + 1) * SIDE].astype(BF16)

    zorder = [4 - near[2], 4 - near[1], 4 - near[0], 0]

    def backward(dys, h):
        half_of = (zh + h) % 2
        firsts = [((y + dy) % 4) * 4 + half_of * 2 for dy in dys]
        whole = jnp.concatenate([adjoints[i] for i in range(blocks)], axis=1)
        lines = [dense[pl.ds(pl.multiple_of(first * SIDE, 2 * SIDE), 2 * SIDE), :] for first in firsts]
        product = lax.dot_general(
            whole, jnp.concatenate(lines, axis=0), (((1,), (1,)), ((), ())), preferred_element_type=F32
        )
        for i, dy in enumerate(dys):
            slot = firsts[i] // 2
            for k in range(2):
                part = product[:, (2 * i + k) * SIDE : (2 * i + k + 1) * SIDE]
                bpart[k, slot] = part.astype(BF16)
            send(f"b_k{dy}{h}", bpart.at[1 - core, slot], bcore.at[slot], to_col(0, 0, 1))

    def over_cores(dy, h):
        slot = ((y + dy) % 4) * 2 + (zh + h) % 2
        arrived(f"b_k{dy}{h}", bcore.at[slot])
        total = bcore[slot].astype(F32) + bpart[core, slot].astype(F32)
        if dy:
            bcore[slot] = total.astype(BF16)
            send(f"b_y{dy}{h}", bcore.at[slot], bring.at[dy - 1, h], to_col(dy, 0, 0))
        else:
            btotal[h] = total

    def ring_sum(h):
        total = btotal[h]
        for dy in (1, 3, 2):
            arrived(f"b_y{dy}{h}", bring.at[dy - 1, h])
            total += bring[dy - 1, h].astype(F32)
        if h:
            bsum[...] = total.astype(BF16)
            send("b_z", bsum, bin_, to_col(0, 1, 0))
        else:
            btotal[0] = total

    def near_sum(i):
        dz = zorder[i]
        block = fpart.at[row_of(1, dz)]
        arrived(f"f_half_up{i}", fhalf_up.at[i])
        block[0:128] = (block[0:128].astype(F32) + fhalf_up[i].astype(F32)).astype(BF16)
        send(f"f_full_up{i}", block, ffull_up.at[i], to_row(1, 0))
        block = fpart.at[row_of(3, dz)]
        arrived(f"f_half_dn{i}", fhalf_down.at[i])
        block[128:256] = (block[128:256].astype(F32) + fhalf_down[i].astype(F32)).astype(BF16)
        send(f"f_full_dn{i}", block, ffull_down.at[i], to_row(3, 0))

    def forward_sum(i):
        arrived(f"f_full_up{i}", ffull_up.at[i])
        arrived(f"f_full_dn{i}", ffull_down.at[i])
        dz = zorder[i]
        total = fpart[row_of(0, dz)].astype(F32) + ffull_up[i].astype(F32) + ffull_down[i].astype(F32)
        if i < 3:
            fsum[i] = total.astype(BF16)
            send("f_z", fsum.at[i], fin.at[dz - 1], to_row(0, dz), dz, 4)
        else:
            ftotal[...] = total

    adjoint_onward(0)
    adjoint_far(0)
    block = states.at[col_of(0, 1, 0)]
    arrived("s_z", block)
    for dy in (2, 1, 3):
        send(f"s_y{dy}1", block, block, to_col(dy, 0, 0))
    send("s_k01", block, block, to_col(0, 0, 1))
    adjoint_onward(1)
    states_over(0)
    adjoint_onward(2)
    adjoint_far(1)
    adjoint_far(2)
    adjoint_far(3)
    states_over(1)
    for h in (0, 1):
        for dy in (0, 1, 3, 2):
            arrived(f"s_k{dy}{h}", states.at[col_of(4 - dy, h, 1)])
    forward(2)
    for i, dz in enumerate(zorder):
        block = fpart.at[row_of(2, dz)]
        send(f"f_half_up{i}", block.at[upper], fhalf_up.at[i], to_row(1, 0))
        send(f"f_half_dn{i}", block.at[lower], fhalf_down.at[i], to_row(3, 0))
    for i in range(4):
        block = adjoints.at[row_of(2, 4 - near[i - 1] if i else 0)]
        if i in STRAIGHT:
            arrived(f"a_x2{i}", block)
        else:
            arrived(f"a_far_up{i}", block.at[upper])
            arrived(f"a_far_dn{i}", block.at[lower])
    backward((2, 1), 1)
    backward((3, 0), 1)
    over_cores(2, 1)
    over_cores(1, 1)
    forward(1)
    forward(3)
    over_cores(3, 1)
    over_cores(0, 1)
    near_sum(0)
    near_sum(1)
    backward((2, 1), 0)
    near_sum(2)
    near_sum(3)
    backward((3, 0), 0)
    over_cores(2, 0)
    over_cores(1, 0)
    over_cores(3, 0)
    over_cores(0, 0)
    ring_sum(1)
    forward(0)
    forward_sum(0)
    forward_sum(1)
    forward_sum(2)
    forward_sum(3)
    ring_sum(0)

    for copy in late_copies:
        copy.wait()
    fed = jnp.dot(input_weight[...], features[...], preferred_element_type=F32)
    total = ftotal[...]
    for d in (1, 2, 3):
        arrived("f_z", fin.at[d - 1], d)
        total += fin[d - 1].astype(F32)
    pre = fed + jnp.dot(mixing[...], total.astype(BF16), preferred_element_type=F32)
    new_state[...] = jnp.tanh(pre).astype(BF16)
    arrived("b_z", bin_)
    back = (btotal[0] + bin_[...].astype(F32)).astype(BF16)
    pulled = lax.dot_general(mixing[...], back, (((0,), (0,)), ((), ())), preferred_element_type=F32)
    own = states[col].astype(F32)
    new_adjoint[...] = ((1.0 - own * own) * (pulled + cotangent[...].astype(F32))).astype(BF16)

    for copy in sent:
        copy.wait_send()
    assert used[0] <= COPIES


def per_device(state, adjoint, features, cotangent, mixing, input_weight, tiles, tile_rows, tile_cols, live_tiles):
    blocks = lax.axis_size("col")
    slab = tiles[0, 0]
    slots = slab.shape[0]
    hidden, nodes = state.shape
    vmem = pl.BlockSpec(memory_space=pltpu.VMEM)
    anywhere = pl.BlockSpec(memory_space=pltpu.HBM)
    block = (hidden, nodes)
    half = (hidden // 2, nodes)
    return pl.pallas_call(
        kernel,
        out_shape=(jax.ShapeDtypeStruct(block, BF16), jax.ShapeDtypeStruct(block, BF16)),
        in_specs=[anywhere] * 10,
        out_specs=(vmem, vmem),
        scratch_shapes=[
            pltpu.VMEM((1, slots), jnp.int32),
            pltpu.VMEM((1, slots), jnp.int32),
            pltpu.SMEM((1, 1), jnp.int32),
            pltpu.VMEM(features.shape, BF16),
            pltpu.VMEM(block, BF16),
            pltpu.VMEM(mixing.shape, BF16),
            pltpu.VMEM(input_weight.shape, BF16),
            pltpu.VMEM((slots + 1, SIDE, SIDE), BF16),
            pltpu.VMEM((blocks * SIDE, blocks * SIDE), BF16),
            pltpu.VMEM((blocks * blocks // SIDE, SIDE), jnp.int32),
            pltpu.SMEM((blocks * blocks // SIDE, SIDE), jnp.int32),
            pltpu.VMEM((blocks, *block), BF16),
            pltpu.VMEM((blocks, *block), BF16),
            pltpu.VMEM((blocks, *block), BF16),
            pltpu.VMEM((4, *half), BF16),
            pltpu.VMEM((4, *half), BF16),
            pltpu.VMEM((4, *block), BF16),
            pltpu.VMEM((4, *block), BF16),
            pltpu.VMEM(block, F32),
            pltpu.VMEM((3, *block), BF16),
            pltpu.VMEM((3, *block), BF16),
            pltpu.VMEM((2, blocks // 2, *block), BF16),
            pltpu.VMEM((blocks // 2, *block), BF16),
            pltpu.VMEM((3, 2, *block), BF16),
            pltpu.VMEM((2, *block), F32),
            pltpu.VMEM(block, BF16),
            pltpu.VMEM(block, BF16),
            pltpu.SemaphoreType.DMA((11,)),
            pltpu.SemaphoreType.DMA((COPIES,)),
            pltpu.SemaphoreType.DMA((COPIES,)),
        ],
        compiler_params=pltpu.CompilerParams(
            collective_id=0, has_side_effects=True, vmem_limit_bytes=26 * 1024 * 1024
        ),
        name="joint_step",
    )(
        *(
            a if a is live_tiles else pltpu.with_memory_space_constraint(a, pltpu.HBM)
            for a in (
                state,
                adjoint,
                slab,
                tile_rows[0],
                tile_cols[0],
                live_tiles,
                features,
                cotangent,
                mixing,
                input_weight,
            )
        )
    )

def solution(mesh):
    placed = (
        P(None, ("row", "col")),
        P(None, ("col", "row")),
        P(None, ("col", "row")),
        P(None, ("row", "col")),
        P(),
        P(),
        P("row", "col", None, None, None),
        P("row", "col", None),
        P("row", "col", None),
        P("row", "col"),
    )
    return jax.shard_map(
        per_device,
        mesh=mesh,
        in_specs=placed,
        out_specs=(P(None, ("col", "row")), P(None, ("row", "col"))),
        check_vma=False,
    )
```
